32 devices in a mesh: blk: 16 (over z, y, core), dp: 2 (over x).
Axes of the slice: x: 2, y: 2, z: 4, core: 2. Of those that a mesh axis runs over, the one named last changes fastest.
Arguments:
- tokens: bfloat16 [4096, 3584], P(('blk', 'dp')), may hold values from -6 to 6
- route_dir: int32 [4096, 1], P(('blk', 'dp')), may hold values from 0 to 2; in each aligned block of 128 rows (0 to 127, 128 to 255, ...) at most 64 rows name the same one
- gate_probs: float32 [4096, 1], P(('blk', 'dp')), may hold values from 0.3 to 1
- gate_weight: bfloat16 [16, 3584, 512], P('blk', 'dp'), may hold values from -0.09375 to 0.09375
- up_weight: bfloat16 [16, 3584, 512], P('blk', 'dp'), may hold values from -0.09375 to 0.09375
- down_weight: bfloat16 [16, 3584, 512], P('blk', 'dp'), may hold values from -0.1875 to 0.1875
Outputs:
- d_tokens: bfloat16 [4096, 3584], P(('blk', 'dp'))
- grad_gate: bfloat16 [16, 3584, 512], P('blk', 'dp')
- grad_up: bfloat16 [16, 3584, 512], P('blk', 'dp')
- grad_down: bfloat16 [16, 3584, 512], P('blk', 'dp')
The draws below stay inside these ranges and needn't reach their ends.
Inputs may be any that keep to these rules, and one draw needn't show every extreme that they name: A token on blk index b sends its row to expert e = (b // 2 + route_dir - 1) mod 8, whose halves sit at blk indices 2e and 2e + 1; on one device at most 64 tokens take the same value.
All inputs are finite; a program needn't handle non-finite values.
Results may differ from the reference program's by a relative error of at most 0.0079.
Values may be sent and summed in bfloat16 or wider, within the bound.
A program may use at most 128 MiB of HBM per device.

```python
import math
import jax
import jax.numpy as jnp
import numpy as np
from jax import lax

D = 3584
FF = 1024
TOK_DEV = 128
HALF = 512
CAP = 64
EXPERTS = 8
TOKENS = 4096
N_BLK = 16
N_DP = 2


def block_levels(stream_key, dims, split, least, largest):
    factor_of = 1.0
    for position, parts in split:
        draws = jax.random.uniform(jax.random.fold_in(jax.random.fold_in(stream_key, 6), position), (parts,), jnp.float32, least / len(split), largest / len(split))
        factor_of = factor_of * jnp.repeat(jnp.exp(draws), dims[position] // parts).reshape((-1,) + (1,) * (len(dims) - 1 - position))
    return factor_of


def deal_out(key, own, number, rows, number_of, top, bound, skew):
    sequence = jax.random.permutation(key, number_of)
    crowded, ordinary = portions_of(number_of, rows * top, bound, skew, True), portions_of(number_of, rows * top, bound, skew, False)
    places = jnp.arange(number_of)

    def named(sizes, rotation):
        used = int((sizes > 0).sum())
        fixed = max(1, used // 4)
        moved = fixed + (places - fixed + rotation * (used - fixed)) % max(1, number_of - fixed)
        return jnp.zeros((number_of,), jnp.int32).at[sequence[jnp.where(places < fixed, places, moved)]].set(jnp.asarray(sizes, jnp.int32))

    sizes = jnp.where(number % 4 == 0, named(crowded, number // 4), named(ordinary, number - number // 4 - 1))
    mixed = jax.random.permutation(jax.random.fold_in(own, 3), number_of)
    donor, taker = mixed[0:number_of // 2 * 2:2], mixed[1:number_of // 2 * 2:2]
    margin = jnp.minimum(sizes[donor] - 1, bound - sizes[taker]) // 2
    margin = jnp.where((donor == sequence[0]) | (taker == sequence[0]) | (sizes[taker] == 0), 0, jnp.maximum(margin, 0))
    moved = jax.random.randint(jax.random.fold_in(own, 4), (number_of // 2,), 0, 1 << 20) % (margin + 1)
    sizes = sizes.at[donor].add(-moved).at[taker].add(moved)
    labels = jnp.searchsorted(jnp.cumsum(sizes), jnp.arange(rows * top), side="right").astype(jnp.int32)
    listing = labels.reshape(top, rows).T
    listing = listing[jax.random.permutation(jax.random.fold_in(own, 1), rows)]
    rotation = jax.random.randint(jax.random.fold_in(own, 2), (rows, 1), 0, top)
    return jnp.take_along_axis(listing, (jnp.arange(top)[None, :] + rotation) % top, axis=1)


def portions_of(number_of, total, bound, slope, full):
    portions = [(1 << 20) // math.isqrt(rank ** slope) + 1 for rank in range(1, number_of + 1)]
    largest = bound if full else min(bound, max(-(-total // number_of), total * portions[0] // sum(portions)))
    least = 1 if total - largest >= number_of - 1 else 0
    counts, surplus = [largest] + [least] * (number_of - 1), total - largest - least * (number_of - 1)
    while surplus > 0:
        free = [i for i in range(1, number_of) if counts[i] < largest] or [i for i in range(1, number_of) if counts[i] < bound]
        whole, remaining = sum([portions[i] for i in free]), surplus
        for i in free:
            more = min(bound - counts[i], max(1, remaining * portions[i] // whole), surplus)
            counts[i] = counts[i] + more
            surplus = surplus - more
    return np.array(counts)


def centred(stream_key, shape, deviation, bound, shards=(), kind=jnp.bfloat16):
    gain = block_levels(stream_key, shape, shards, -0.22, 0.18) if shards else 1.0
    values = jax.random.normal(stream_key, shape, jnp.float32) * deviation * gain
    return jnp.minimum(jnp.maximum(values, -bound), bound).astype(kind)


def setup_inputs(seed: int = 0) -> dict:
    keys = jax.random.split(jax.random.key(seed), 7)
    tokens = centred(keys[0], (TOKENS, D), 1.0, 6.0, ((0, 32),))
    route_dir_keys = jax.random.split(jax.random.fold_in(keys[1], 1), TOKENS // TOK_DEV)
    route_dir_turns = jax.random.permutation(jax.random.fold_in(keys[1], 3), TOKENS // TOK_DEV)
    route_dir = jax.vmap(lambda own, number: deal_out(jax.random.fold_in(keys[1], 2), own, number, TOK_DEV, 3, 1, CAP, 2))(route_dir_keys, route_dir_turns).reshape((TOKENS, 1))
    gate_probs = jnp.clip(0.3 + 0.7 * jax.random.uniform(keys[2], (TOKENS, 1), jnp.float32) ** block_levels(keys[2], (TOKENS, 1), ((0, 32),), -0.2, 0.2), 0.3, 1.0)
    gate_weight = centred(keys[3], (2 * EXPERTS, D, HALF), D ** -0.5, 0.09375, ((0, 16), (1, 2)))
    up_weight = centred(keys[4], (2 * EXPERTS, D, HALF), D ** -0.5, 0.09375, ((0, 16), (1, 2)))
    down_weight = centred(keys[5], (2 * EXPERTS, D, HALF), FF ** -0.5, 0.1875, ((0, 16), (1, 2)))
    return {"tokens": tokens, "route_dir": route_dir, "gate_probs": gate_probs, "gate_weight": gate_weight, "up_weight": up_weight, "down_weight": down_weight}


def selection(directions, capacity):
    slot_ids = jnp.arange(capacity, dtype=jnp.int32)
    planes = []
    for direction in range(3):
        chosen = (directions == direction).astype(jnp.int32)
        places = jnp.cumsum(chosen, axis=-1, dtype=jnp.int32) - 1
        matches = (chosen[..., None, :] == 1) & (places[..., None, :] == slot_ids[:, None])
        planes.append(matches)
    return jnp.stack(planes, axis=-3).astype(jnp.bfloat16)

def round_trip(payload):
    return lax.optimization_barrier(payload.astype(jnp.bfloat16)).astype(jnp.float32)

def matmul(left_side, right_side):
    return jnp.dot(left_side, right_side, preferred_element_type=jnp.float32)

def times_transposed(left_side, right_side):
    return lax.dot_general(left_side, right_side, (((1,), (1,)), ((), ())), preferred_element_type=jnp.float32)

def activate(pre_gate, pre_up):
    sigmoid = jax.nn.sigmoid(pre_gate)
    return ((pre_gate * sigmoid * pre_up).astype(jnp.bfloat16), sigmoid)

def hidden_grads(d_hidden, pre_gate, pre_up, sigmoid):
    d_gate = (d_hidden * pre_up * (sigmoid * (1.0 + pre_gate * (1.0 - sigmoid)))).astype(jnp.bfloat16)
    d_up = (d_hidden * (pre_gate * sigmoid)).astype(jnp.bfloat16)
    return (d_gate, d_up)

def group_grad(left_side, right_side, groups):
    lhs_float = left_side.reshape(groups, -1, left_side.shape[-1]).astype(jnp.float32)
    rhs_float = right_side.reshape(groups, -1, right_side.shape[-1]).astype(jnp.float32)
    group_terms = jnp.einsum('grk,grh->gkh', lhs_float, rhs_float)
    return lax.optimization_barrier(jnp.sum(round_trip(group_terms), axis=0)).astype(jnp.bfloat16)

def reference(tokens, route_dir, gate_probs, gate_weight, up_weight, down_weight):
    blocks = tokens.reshape(N_BLK, N_DP, TOK_DEV, D)
    directions = route_dir.reshape(N_BLK, N_DP, TOK_DEV)
    weights_in = gate_probs.reshape(N_BLK, N_DP, TOK_DEV)
    selector = selection(directions, CAP)
    offsets = jnp.array([2, 3, 0, 1, -2, -1], dtype=jnp.int32)
    side_ids = jnp.array([0, 0, 1, 1, 2, 2], dtype=jnp.int32)
    row_count = N_DP * 6 * CAP

    def one_expert(expert):
        sources = (offsets + 2 * expert) % N_BLK
        chosen = selector[sources, :, side_ids].astype(jnp.float32)
        gathered = jnp.einsum('ndst,ndtk->ndsk', chosen, blocks[sources].astype(jnp.float32)).astype(jnp.bfloat16)
        scales = jnp.einsum('ndst,ndt->nds', chosen, weights_in[sources])
        inputs = gathered.transpose(1, 0, 2, 3).reshape(row_count, D)
        scales = scales.transpose(1, 0, 2).reshape(row_count, 1)
        stored = []
        partial_sum = jnp.zeros((row_count, D), jnp.float32)
        for which_half in range(2):
            member = 2 * expert + which_half
            w_gate = lax.dynamic_index_in_dim(gate_weight, member, 0, keepdims=False)
            w_up = lax.dynamic_index_in_dim(up_weight, member, 0, keepdims=False)
            w_down = lax.dynamic_index_in_dim(down_weight, member, 0, keepdims=False)
            pre_gate = matmul(inputs, w_gate)
            pre_up = matmul(inputs, w_up)
            activated, sigmoid = activate(pre_gate, pre_up)
            partial_sum = partial_sum + round_trip(times_transposed(activated, w_down))
            stored.append((w_gate, w_up, w_down, pre_gate, pre_up, activated, sigmoid))
        result = scales * round_trip(partial_sum)
        back_rows = (scales * result).astype(jnp.bfloat16)
        grads_gate = []
        grads_up = []
        grads_down = []
        dx_sum = jnp.zeros((row_count, D), jnp.float32)
        for w_gate, w_up, w_down, pre_gate, pre_up, activated, sigmoid in stored:
            d_hidden = matmul(back_rows, w_down)
            d_gate, d_up = hidden_grads(d_hidden, pre_gate, pre_up, sigmoid)
            grads_gate.append(group_grad(inputs, d_gate, N_DP))
            grads_up.append(group_grad(inputs, d_up, N_DP))
            grads_down.append(group_grad(back_rows, activated, N_DP))
            dx_sum = dx_sum + round_trip(times_transposed(d_gate, w_gate) + times_transposed(d_up, w_up))
        dx_rows = dx_sum.astype(jnp.bfloat16).reshape(N_DP, 6, CAP, D).transpose(1, 0, 2, 3)
        return (dx_rows, jnp.stack(grads_gate), jnp.stack(grads_up), jnp.stack(grads_down))
    dx_rows, grads_gate, grads_up, grads_down = lax.map(one_expert, jnp.arange(EXPERTS, dtype=jnp.int32))

    def one_source(source):
        pieces = []
        for direction in range(3):
            expert = (source // 2 + direction - 1) % EXPERTS
            slot_id = 2 * direction + source % 2
            pieces.append(dx_rows[expert, slot_id])
        stacked = jnp.stack(pieces, axis=1)
        return jnp.einsum('djst,djsk->dtk', selector[source].astype(jnp.float32), stacked.astype(jnp.float32)).astype(jnp.bfloat16)
    d_tokens = lax.map(one_source, jnp.arange(N_BLK, dtype=jnp.int32)).reshape(TOKENS, D)
    shape_out = (2 * EXPERTS, D, HALF)
    return (d_tokens, grads_gate.reshape(shape_out), grads_up.reshape(shape_out), grads_down.reshape(shape_out))
```

```python
import jax
import jax.numpy as jnp
from jax import lax
from jax.sharding import PartitionSpec as P

CAP = 64


def shifted(shard, axis, by):
    length = lax.axis_size(axis)
    return lax.ppermute(shard, axis, [(i, (i + by) % length) for i in range(length)])


def partner_2(block, axis, bit):
    count = lax.axis_size(axis)
    route = []
    for low in range(count):
        high = low | 1 << bit
        if high != low and high < count:
            route += [(low, high), (high, low)]
    return lax.ppermute(block, axis, route)


def selection(directions, capacity):
    slot_ids = jnp.arange(capacity, dtype=jnp.int32)
    planes = []
    for direction in range(3):
        chosen = (directions == direction).astype(jnp.int32)
        places = jnp.cumsum(chosen, axis=-1, dtype=jnp.int32) - 1
        matches = (chosen[..., None, :] == 1) & (places[..., None, :] == slot_ids[:, None])
        planes.append(matches)
    return jnp.stack(planes, axis=-3).astype(jnp.bfloat16)


def matmul(left_side, right_side):
    return jnp.dot(left_side, right_side, preferred_element_type=jnp.float32)


def times_transposed(left_side, right_side):
    return lax.dot_general(
        left_side, right_side, (((1,), (1,)), ((), ())), preferred_element_type=jnp.float32
    )


def transposed_times(left_side, right_side):
    return lax.dot_general(
        left_side, right_side, (((0,), (0,)), ((), ())), preferred_element_type=jnp.float32
    )


def activate(pre_gate, pre_up):
    sigmoid = jax.nn.sigmoid(pre_gate)
    return ((pre_gate * sigmoid * pre_up).astype(jnp.bfloat16), sigmoid)


def hidden_grads(d_hidden, pre_gate, pre_up, sigmoid):
    d_gate = (d_hidden * pre_up * (sigmoid * (1.0 + pre_gate * (1.0 - sigmoid)))).astype(
        jnp.bfloat16
    )
    d_up = (d_hidden * (pre_gate * sigmoid)).astype(jnp.bfloat16)
    return (d_gate, d_up)


def to_lower(payload):
    return shifted(payload, "blk", -2)


def to_upper(payload):
    return shifted(payload, "blk", 2)


def partner(payload):
    return partner_2(payload, "blk", 0)


def unpack(selector, rows_back):
    return jnp.einsum("jst,jsd->td", selector, rows_back, preferred_element_type=jnp.float32)


def select_rows(selector, source_rows):
    return jnp.einsum(
        "jst,td->jsd", selector, source_rows, preferred_element_type=jnp.float32
    ).astype(jnp.bfloat16)


def other_group(payload):
    return partner_2(payload, "dp", 0)


def groups_swapped(payload):
    rows = payload.shape[0] // 2
    return jnp.concatenate([payload[rows:], payload[:rows]])


def sides_swapped(payload):
    blocks = payload.reshape(2, 2, CAP, payload.shape[-1])
    return jnp.stack([blocks[:, 1], blocks[:, 0]], axis=1).reshape(payload.shape)


def same(payload):
    return payload


def joined(local):
    return jnp.stack([local, partner(local)], axis=1).reshape((-1,) + local.shape[2:])


def per_device(tokens, route_dir, gate_probs, gate_weight, up_weight, down_weight):
    w_gate, w_up, w_down = gate_weight[0], up_weight[0], down_weight[0]
    half = w_gate.shape[0]
    here = lax.axis_index("dp")

    theirs = other_group(lax.dynamic_slice_in_dim(tokens, (1 - here) * half, half, axis=1))
    mine = lax.dynamic_slice_in_dim(tokens, here * half, half, axis=1)
    facts = jnp.stack([route_dir[:, 0].astype(jnp.float32), gate_probs[:, 0]])
    facts_theirs = other_group(facts)
    selectors = (
        selection(route_dir[:, 0], CAP),
        selection(facts_theirs[0].astype(jnp.int32), CAP),
    )
    picked = (select_rows(selectors[0], mine), select_rows(selectors[1], theirs))
    slot_gates = jnp.stack(
        [
            jnp.sum(selectors[0].astype(jnp.float32) * facts[1], axis=-1),
            jnp.sum(selectors[1].astype(jnp.float32) * facts_theirs[1], axis=-1),
        ],
        axis=1,
    )
    outward, homeward = (to_lower, same, to_upper), (to_upper, same, to_lower)
    gates_here = jnp.stack([outward[j](slot_gates[j]) for j in range(3)])
    gates_there = partner(gates_here)
    gates = jnp.stack([gates_here, gates_there], axis=2).reshape(3, -1, 1)

    rows, hidden, back, down_gate, down_up, home = {}, {}, {}, {}, {}, {}
    saved = {}
    order = (1, 0, 2)
    for j in order:
        local = jnp.stack([outward[j](picked[0][j]), outward[j](picked[1][j])])
        rows[j] = joined(local)
    for j in order:
        part_gate = matmul(rows[j], w_gate)
        part_up = matmul(rows[j], w_up)
        sent = jnp.concatenate([part_gate, part_up], axis=1).astype(jnp.bfloat16)
        received = other_group(groups_swapped(sent)).astype(jnp.float32)
        pre_gate = part_gate + received[:, : part_gate.shape[1]]
        pre_up = part_up + received[:, part_gate.shape[1] :]
        hidden[j], sigmoid = activate(pre_gate, pre_up)
        saved[j] = (pre_gate, pre_up, sigmoid)
    for j in order:
        partial_value = times_transposed(hidden[j], w_down).astype(jnp.bfloat16)
        received = partner(sides_swapped(partial_value))
        expert_out = (
            partial_value.astype(jnp.float32) + received.astype(jnp.float32)
        ).astype(jnp.bfloat16)
        back[j] = (gates[j] * (gates[j] * expert_out)).astype(jnp.bfloat16)
    for j in (0, 2, 1):
        part_hidden = matmul(back[j], w_down)
        received = other_group(groups_swapped(part_hidden.astype(jnp.bfloat16)))
        d_hidden = part_hidden + received.astype(jnp.float32)
        down_gate[j], down_up[j] = hidden_grads(d_hidden, *saved[j])
        dx_part = (
            times_transposed(down_gate[j], w_gate) + times_transposed(down_up[j], w_up)
        ).astype(jnp.bfloat16)
        blocks = dx_part.reshape(2, 2, CAP, half)
        received = partner(blocks[:, 1])
        combined = (
            blocks[:, 0].astype(jnp.float32) + received.astype(jnp.float32)
        ).astype(jnp.bfloat16)
        home[j] = homeward[j](combined)

    def all_rows(of):
        return jnp.concatenate([of[j] for j in range(3)])

    every_row = all_rows(rows)
    grad_down = transposed_times(all_rows(back), all_rows(hidden)).astype(jnp.bfloat16)[None]
    grad_gate = transposed_times(every_row, all_rows(down_gate)).astype(jnp.bfloat16)[None]
    grad_up = transposed_times(every_row, all_rows(down_up)).astype(jnp.bfloat16)[None]

    d_mine, d_theirs = [
        unpack(selectors[g], jnp.stack([home[j][g] for j in range(3)])).astype(jnp.bfloat16)
        for g in range(2)
    ]
    d_rest = other_group(d_theirs)
    first = here == 0
    d_tokens = jnp.concatenate(
        [jnp.where(first, d_mine, d_rest), jnp.where(first, d_rest, d_mine)], axis=1
    )
    return (d_tokens, grad_gate, grad_up, grad_down)


def solution(mesh):
    return jax.shard_map(
        per_device,
        mesh=mesh,
        in_specs=(
            P(("blk", "dp"), None),
            P(("blk", "dp"), None),
            P(("blk", "dp"), None),
            P("blk", "dp", None),
            P("blk", "dp", None),
            P("blk", "dp", None),
        ),
        out_specs=(
            P(("blk", "dp"), None),
            P("blk", "dp", None),
            P("blk", "dp", None),
            P("blk", "dp", None),
        ),
        check_vma=False,
    )
```

```python
import jax
import jax.numpy as jnp
from jax import lax
from jax.sharding import PartitionSpec as P


CAP = 64


def shifted(shard, axis, by):
    length = lax.axis_size(axis)
    return lax.ppermute(shard, axis, [(i, (i + by) % length) for i in range(length)])


def partner_2(block, axis, bit):
    count = lax.axis_size(axis)
    route = []
    for low in range(count):
        high = low | 1 << bit
        if high != low and high < count:
            route += [(low, high), (high, low)]
    return lax.ppermute(block, axis, route)


def selection(directions, capacity):
    slot_ids = jnp.arange(capacity, dtype=jnp.int32)
    planes = []
    for direction in range(3):
        chosen = (directions == direction).astype(jnp.int32)
        places = jnp.cumsum(chosen, axis=-1, dtype=jnp.int32) - 1
        matches = (chosen[..., None, :] == 1) & (places[..., None, :] == slot_ids[:, None])
        planes.append(matches)
    return jnp.stack(planes, axis=-3).astype(jnp.bfloat16)


def matmul(left_side, right_side):
    return jnp.dot(left_side, right_side, preferred_element_type=jnp.float32)


def times_transposed(left_side, right_side):
    return lax.dot_general(
        left_side, right_side, (((1,), (1,)), ((), ())), preferred_element_type=jnp.float32
    )


def transposed_times(left_side, right_side):
    return lax.dot_general(
        left_side, right_side, (((0,), (0,)), ((), ())), preferred_element_type=jnp.float32
    )


def activate(pre_gate, pre_up):
    sigmoid = jax.nn.sigmoid(pre_gate)
    return ((pre_gate * sigmoid * pre_up).astype(jnp.bfloat16), sigmoid)


def hidden_grads(d_hidden, pre_gate, pre_up, sigmoid):
    d_gate = (d_hidden * pre_up * (sigmoid * (1.0 + pre_gate * (1.0 - sigmoid)))).astype(
        jnp.bfloat16
    )
    d_up = (d_hidden * (pre_gate * sigmoid)).astype(jnp.bfloat16)
    return (d_gate, d_up)


def to_lower(payload):
    return shifted(payload, "blk", -2)


def to_upper(payload):
    return shifted(payload, "blk", 2)


def partner(payload):
    return partner_2(payload, "blk", 0)


def unpack(selector, rows_back):
    return jnp.einsum("jst,jsd->td", selector, rows_back, preferred_element_type=jnp.float32)


def select_rows(selector, source_rows):
    return jnp.einsum(
        "jst,td->jsd", selector, source_rows, preferred_element_type=jnp.float32
    ).astype(jnp.bfloat16)


def other_group(payload):
    return partner_2(payload, "dp", 0)


def groups_swapped(payload):
    rows = payload.shape[0] // 2
    return jnp.concatenate([payload[rows:], payload[:rows]])


def sides_swapped(payload):
    blocks = payload.reshape(2, 2, CAP, payload.shape[-1])
    return jnp.stack([blocks[:, 1], blocks[:, 0]], axis=1).reshape(payload.shape)


def same(payload):
    return payload


def joined(local):
    return jnp.stack([local, partner(local)], axis=1).reshape((-1,) + local.shape[2:])


def per_device(tokens, route_dir, gate_probs, gate_weight, up_weight, down_weight):
    w_gate, w_up, w_down = gate_weight[0], up_weight[0], down_weight[0]
    half = w_gate.shape[0]
    here = lax.axis_index("dp")

    theirs = other_group(lax.dynamic_slice_in_dim(tokens, (1 - here) * half, half, axis=1))
    mine = lax.dynamic_slice_in_dim(tokens, here * half, half, axis=1)
    facts = jnp.stack([route_dir[:, 0].astype(jnp.float32), gate_probs[:, 0]])
    facts_theirs = other_group(facts)
    selectors = (
        selection(route_dir[:, 0], CAP),
        selection(facts_theirs[0].astype(jnp.int32), CAP),
    )
    picked = []
    for g, features in enumerate((mine, theirs)):
        picked.append(select_rows(selectors[g], features))
    slot_gates = jnp.stack(
        [
            jnp.sum(selectors[0].astype(jnp.float32) * facts[1], axis=-1),
            jnp.sum(selectors[1].astype(jnp.float32) * facts_theirs[1], axis=-1),
        ],
        axis=1,
    )
    outward, homeward = (to_lower, same, to_upper), (to_upper, same, to_lower)
    gates_here = jnp.stack([outward[j](slot_gates[j]) for j in range(3)])
    gates_there = partner(gates_here)
    gates = jnp.stack([gates_here, gates_there], axis=2).reshape(3, -1, 1)

    rows, hidden, back, down_gate, down_up, home = {}, {}, {}, {}, {}, {}
    saved = {}
    order = (1, 0, 2)
    for j in order:
        local = jnp.stack([outward[j](picked[g][j]) for g in range(2)])
        rows[j] = joined(local)
    for j in order:
        part_gate = matmul(rows[j], w_gate)
        part_up = matmul(rows[j], w_up)
        sent = jnp.concatenate([part_gate, part_up], axis=1).astype(jnp.bfloat16)
        sent = groups_swapped(sent)
        received = other_group(sent).astype(jnp.float32)
        pre_gate = part_gate + received[:, : part_gate.shape[1]]
        pre_up = part_up + received[:, part_gate.shape[1] :]
        hidden[j], sigmoid = activate(pre_gate, pre_up)
        saved[j] = (pre_gate, pre_up, sigmoid)
    for j in order:
        partial_value = times_transposed(hidden[j], w_down).astype(jnp.bfloat16)
        received = partner(sides_swapped(partial_value))
        expert_out = (
            partial_value.astype(jnp.float32) + received.astype(jnp.float32)
        ).astype(jnp.bfloat16)
        back[j] = (gates[j] * (gates[j] * expert_out)).astype(jnp.bfloat16)
    for j in (0, 2, 1):
        part_hidden = matmul(back[j], w_down)
        sent = groups_swapped(part_hidden.astype(jnp.bfloat16))
        received = other_group(sent)
        d_hidden = part_hidden + received.astype(jnp.float32)
        down_gate[j], down_up[j] = hidden_grads(d_hidden, *saved[j])
        dx_part = (
            times_transposed(down_gate[j], w_gate) + times_transposed(down_up[j], w_up)
        ).astype(jnp.bfloat16)
        blocks = dx_part.reshape(2, 2, CAP, half)
        received = partner(blocks[:, 1])
        combined = (
            blocks[:, 0].astype(jnp.float32) + received.astype(jnp.float32)
        ).astype(jnp.bfloat16)
        home[j] = [homeward[j](combined[g]) for g in range(2)]

    def all_rows(of):
        return jnp.concatenate([of[j] for j in range(3)])

    every_row = all_rows(rows)
    grad_down = transposed_times(all_rows(back), all_rows(hidden)).astype(jnp.bfloat16)[None]
    grad_gate = transposed_times(every_row, all_rows(down_gate)).astype(jnp.bfloat16)[None]
    grad_up = transposed_times(every_row, all_rows(down_up)).astype(jnp.bfloat16)[None]

    results = []
    for g in range(2):
        results.append(
            unpack(selectors[g], jnp.stack([home[j][g] for j in range(3)])).astype(
                jnp.bfloat16
            )
        )
    d_mine, d_theirs = results
    d_rest = other_group(d_theirs)
    first = here == 0
    d_tokens = jnp.concatenate(
        [jnp.where(first, d_mine, d_rest), jnp.where(first, d_rest, d_mine)], axis=1
    )
    return (d_tokens, grad_gate, grad_up, grad_down)


def solution(mesh):
    return jax.shard_map(
        per_device,
        mesh=mesh,
        in_specs=(
            P(("blk", "dp"), None),
            P(("blk", "dp"), None),
            P(("blk", "dp"), None),
            P("blk", "dp", None),
            P("blk", "dp", None),
            P("blk", "dp", None),
        ),
        out_specs=(
            P(("blk", "dp"), None),
            P("blk", "dp", None),
            P("blk", "dp", None),
            P("blk", "dp", None),
        ),
        check_vma=False,
    )
```
